32 devices in a mesh: groups: 2 (over y), wide: 8 (over z, x), narrow: 2 (over core).
Axes of the slice: x: 2, y: 2, z: 4, core: 2. Of those that a mesh axis runs over, the one named last changes fastest.
Arguments:
- queries: bfloat16 [16384, 1024], P(('groups', 'wide', 'narrow')), parts along dimension 0, may hold values from -6 to 6
- latents: bfloat16 [256, 1024], P(('groups', 'wide', 'narrow')), parts along dimension 0
- norm_gains: float32 [2, 1024], replicated, may hold values from 0.5 to 1.5
- q_weight: bfloat16 [2, 1024, 1024], P(None, 'narrow'), may hold values from -0.1875 to 0.1875
- k_weight: bfloat16 [2, 1024, 1024], P(None, 'narrow'), may hold values from -0.1875 to 0.1875
- v_weight: bfloat16 [2, 1024, 1024], P(None, 'narrow'), may hold values from -0.1875 to 0.1875
- o_weight: bfloat16 [2, 1024, 1024], P(None, 'narrow'), may hold values from -0.1875 to 0.1875
Outputs:
- decoded: bfloat16 [16384, 1024], P(('groups', 'wide', 'narrow')), parts along dimension 0
The draws below stay inside these ranges and needn't reach their ends.
There are 2 independent parts, one for each index of `groups`. The reference program is written for one: setup_inputs(seed, part) draws one part's arguments, and reference() takes and returns one part's arrays. A program takes and returns all parts, laid end to end along the dimension named above; an argument that names none is the same for every part. Nothing has to cross between parts.
All inputs are finite; a program needn't handle non-finite values.
Results may differ from the reference program's by a relative error of at most 0.025.
The reference program's roundings to bfloat16 on the way (of `hidden`, `key_rows`, `normed`, `query_rows`, `probs` and `attended`) count: a program that leaves them out, or rounds other values in their place, can miss the bound.
Values may be sent and summed in bfloat16 or wider, within the bound.
A program may use at most 128 MiB of HBM per device.

```python
import math
import jax
import jax.numpy as jnp
from jax import lax

D = 1024
HEADS = 16
LAYERS = 2
QUERIES = 8192
LATENT = 128


def draw_latents(key, part):
    return jnp.clip(2.5 * jax.random.normal(key, (LATENT, D), jnp.float32), -12.0, 12.0).astype(jnp.bfloat16)


def level_of(own_key, shape, pieces, low, top_value):
    def one(dim, parts):
        draws = jax.random.uniform(jax.random.fold_in(jax.random.fold_in(own_key, 6), dim), (parts,), jnp.float32, low / len(pieces), top_value / len(pieces))
        return jnp.repeat(jnp.exp(draws), shape[dim] // parts).reshape((-1,) + (1,) * (len(shape) - dim - 1))

    loudness = one(*pieces[0])
    for cut in pieces[1:]:
        loudness = loudness * one(*cut)
    return loudness


def bell_draw(stream_key, shape, scale, most, pieces=(), dtype=jnp.bfloat16):
    values = jax.random.normal(stream_key, shape, jnp.float32) * scale
    if len(pieces) > 0:
        values = level_of(stream_key, shape, pieces, -0.22, 0.18) * values
    return jnp.clip(values, min=-most, max=most).astype(dtype)


def setup_inputs(seed: int = 0, part: int = 0) -> dict:
    arg_keys = jax.random.split(jax.random.key(seed), 8)
    part_splits = jax.random.split(jax.random.fold_in(arg_keys[7], part), 8)
    queries = bell_draw(part_splits[0], (QUERIES, D), 1.0, 6.0, ((0, 16),))
    latents = draw_latents(jax.random.fold_in(jax.random.fold_in(arg_keys[7], part), 71), part)
    norm_gains = jnp.clip(1.0 + 0.1 * jax.random.normal(arg_keys[2], (LAYERS, D), jnp.float32), 0.5, 1.5)
    q_weight = bell_draw(arg_keys[3], (LAYERS, D, D), D ** -0.5, 0.1875, ((1, 2),))
    k_weight = bell_draw(arg_keys[4], (LAYERS, D, D), D ** -0.5, 0.1875, ((1, 2),))
    v_weight = bell_draw(arg_keys[5], (LAYERS, D, D), D ** -0.5, 0.1875, ((1, 2),))
    o_weight = bell_draw(arg_keys[6], (LAYERS, D, D), D ** -0.5, 0.1875, ((1, 2),))
    return {"queries": queries, "latents": latents, "norm_gains": norm_gains, "q_weight": q_weight, "k_weight": k_weight, "v_weight": v_weight, "o_weight": o_weight}


def layer_norm(row_data, gain):
    values = row_data.astype(jnp.float32)
    center = values - lax.optimization_barrier(jnp.mean(values, axis=-1, keepdims=True))
    spread = lax.optimization_barrier(jnp.mean(center * center, axis=-1, keepdims=True))
    return (center * lax.rsqrt(spread + 1e-05) * gain).astype(jnp.bfloat16)

def attend_block(query_block, key_rows, value_rows):
    block_rows = query_block.shape[0]
    head_size = D // HEADS
    query_heads = query_block.astype(jnp.float32).reshape(block_rows, HEADS, head_size)
    key_heads = key_rows.astype(jnp.float32).reshape(LATENT, HEADS, head_size)
    value_heads = value_rows.astype(jnp.float32).reshape(LATENT, HEADS, head_size)
    scores = jnp.einsum('qhd,khd->hqk', query_heads, key_heads)
    row_max = lax.optimization_barrier(jnp.max(scores, axis=-1, keepdims=True))
    expo = jnp.exp(scores - row_max)
    row_sum = lax.optimization_barrier(jnp.sum(expo, axis=-1))
    probs = lax.optimization_barrier(expo.astype(jnp.bfloat16)).astype(jnp.float32)
    weighted = jnp.einsum('hqk,khd->qhd', probs, value_heads)
    weighted = weighted / jnp.transpose(row_sum)[:, :, None]
    return weighted.reshape(block_rows, D).astype(jnp.bfloat16)

def reference(queries, latents, norm_gains, q_weight, k_weight, v_weight, o_weight):
    head_size = D // HEADS
    score_scale = head_size ** (-0.5)
    block_rows = math.gcd(QUERIES, 512)
    hidden = queries
    for layer_index in range(LAYERS):
        key_rows = jnp.dot(latents, k_weight[layer_index], preferred_element_type=jnp.float32).astype(jnp.bfloat16)
        value_rows = jnp.dot(latents, v_weight[layer_index], preferred_element_type=jnp.float32).astype(jnp.bfloat16)
        normed = layer_norm(hidden, norm_gains[layer_index])
        query_rows = (jnp.dot(normed, q_weight[layer_index], preferred_element_type=jnp.float32) * score_scale).astype(jnp.bfloat16)
        query_blocks = query_rows.reshape(QUERIES // block_rows, block_rows, D)
        attended = lax.map(lambda query_block: attend_block(query_block, key_rows, value_rows), query_blocks)
        attended = attended.reshape(QUERIES, D)
        output_rows = jnp.dot(attended, o_weight[layer_index], preferred_element_type=jnp.float32)
        hidden = (hidden.astype(jnp.float32) + output_rows).astype(jnp.bfloat16)
    return hidden
```

```python
import functools

import jax
import jax.numpy as jnp
from jax import lax
from jax.experimental import pallas as pl
from jax.experimental.pallas import tpu as pltpu
from jax.sharding import PartitionSpec as P

HEADS = 16
LAYERS = 2
MESH = pl.DeviceIdType.MESH
F32 = jnp.float32
BF16 = jnp.bfloat16


def decoder(
    wide,
    narrow,
    queries,
    latents,
    gains,
    q_weight,
    k_weight,
    v_weight,
    o_weight,
    out,
    hidden,
    normed,
    query_rows,
    attended,
    lat,
    lat_rows,
    wq,
    wo,
    wk,
    wv,
    own_sums,
    peer_sums,
    local_sem,
    lat_local_sem,
    weight_local_sem,
    lat_send_sem,
    lat_recv_sem,
    weight_send_sem,
    weight_recv_sem,
    sums_send_sem,
    sums_recv_sem,
):
    devices = wide * narrow
    w = lax.axis_index("wide")
    n = lax.axis_index("narrow")
    me = w * narrow + n
    rows, width = hidden.shape
    half = wk.shape[1]
    lat_count = lat_rows.shape[0]
    head_size = width // HEADS
    pair = 2 * head_size
    scale = head_size ** (-0.5)
    my_half = pl.ds(pl.multiple_of(n * half, half), half)
    peer = {"narrow": 1 - n}

    local = [pltpu.make_async_copy(queries, hidden, local_sem)]
    own_latents = pltpu.make_async_copy(latents.at[:, my_half], lat.at[me], lat_local_sem)
    own = {}
    for layer in range(LAYERS):
        own["q", layer] = pltpu.make_async_copy(
            q_weight.at[layer], wq.at[layer, my_half], weight_local_sem.at[0, layer]
        )
        own["o", layer] = pltpu.make_async_copy(
            o_weight.at[layer], wo.at[layer, my_half], weight_local_sem.at[1, layer]
        )
        own["k", layer] = pltpu.make_async_copy(
            k_weight.at[layer], wk.at[layer], weight_local_sem.at[2, layer]
        )
        own["v", layer] = pltpu.make_async_copy(
            v_weight.at[layer], wv.at[layer], weight_local_sem.at[3, layer]
        )
    local[0].start()
    own_latents.start()
    for layer in range(LAYERS):
        for name in "kvqo":
            own[name, layer].start()

    barrier = pltpu.get_barrier_semaphore()

    def greet(step, carry):
        other = lax.rem(me + step, devices)
        pl.semaphore_signal(
            barrier,
            inc=1,
            device_id={"wide": other // narrow, "narrow": lax.rem(other, narrow)},
            device_id_type=MESH,
        )
        return carry

    lax.fori_loop(1, devices, greet, 0)
    pl.semaphore_wait(barrier, devices - 1)

    def latent_copy(step):
        other = lax.rem(me + step, devices)
        other_n = lax.rem(other, narrow)
        columns = pl.ds(pl.multiple_of(other_n * half, half), half)
        return pltpu.make_async_remote_copy(
            src_ref=latents.at[:, columns],
            dst_ref=lat.at[me],
            send_sem=lat_send_sem.at[step],
            recv_sem=lat_recv_sem.at[me],
            device_id={"wide": other // narrow, "narrow": other_n},
            device_id_type=MESH,
        )

    def send_latents(step, carry):
        latent_copy(step).start()
        return carry

    lax.fori_loop(1, devices, send_latents, 0)

    def weight_copy(index, layer):
        source, target = ((q_weight, wq), (o_weight, wo))[index]
        return pltpu.make_async_remote_copy(
            src_ref=source.at[layer],
            dst_ref=target.at[layer, my_half],
            send_sem=weight_send_sem.at[index, layer],
            recv_sem=weight_recv_sem.at[index, layer],
            device_id=peer,
            device_id_type=MESH,
        )

    def sums_copy(index, layer):
        return pltpu.make_async_remote_copy(
            src_ref=own_sums.at[layer, index],
            dst_ref=peer_sums.at[layer, index],
            send_sem=sums_send_sem.at[index, layer],
            recv_sem=sums_recv_sem.at[index, layer],
            device_id=peer,
            device_id_type=MESH,
        )

    weight_copy(0, 0).start()

    norm_rows = min(rows, 128)

    def layer_norm(layer):
        gain = gains[layer : layer + 1, :]

        def chunk(index, carry):
            piece = pl.ds(pl.multiple_of(index * norm_rows, norm_rows), norm_rows)
            values = hidden[piece, :].astype(F32)
            center = values - jnp.mean(values, axis=-1, keepdims=True)
            spread = jnp.mean(center * center, axis=-1, keepdims=True)
            normed[piece, :] = (center * lax.rsqrt(spread + 1e-05) * gain).astype(BF16)
            return carry

        lax.fori_loop(0, rows // norm_rows, chunk, 0)

    sum_rows = min(lat_count, 256)
    tile = 256

    def project_latents(index, layer):
        panel = (wk, wv)[index]

        def chunk(step, carry):
            row = step // (width // tile)
            col = lax.rem(step, width // tile)
            piece = pl.ds(pl.multiple_of(row * sum_rows, sum_rows), sum_rows)
            columns = pl.ds(pl.multiple_of(col * tile, tile), tile)
            own_sums[layer, index, piece, columns] = jnp.dot(
                lat_rows[piece, :], panel[layer, :, columns], preferred_element_type=F32
            )
            return carry

        lax.fori_loop(0, (lat_count // sum_rows) * (width // tile), chunk, 0)

    def project_queries(layer):
        def chunk(col, carry):
            columns = pl.ds(pl.multiple_of(col * tile, tile), tile)
            sums = jnp.dot(normed[...], wq[layer, :, columns], preferred_element_type=F32)
            query_rows[:, columns] = (sums * scale).astype(BF16)
            return carry

        lax.fori_loop(0, width // tile, chunk, 0)

    def project_output(layer, target):
        def chunk(col, carry):
            columns = pl.ds(pl.multiple_of(col * tile, tile), tile)
            sums = jnp.dot(attended[...], wo[layer, :, columns], preferred_element_type=F32)
            target[:, columns] = (hidden[:, columns].astype(F32) + sums).astype(BF16)
            return carry

        lax.fori_loop(0, width // tile, chunk, 0)

    attend_rows = rows if lat_count <= 256 else min(rows, 128)

    def attend(layer):
        first = lax.broadcasted_iota(jnp.int32, (lat_count, pair), 1) < head_size
        zeros = jnp.zeros((lat_count, pair), F32)
        ones = jnp.ones((lat_count, pair), F32)
        counts = jnp.concatenate(
            [jnp.where(first, ones, zeros), jnp.where(first, zeros, ones)], axis=0
        ).astype(BF16)

        def heads(index, carry):
            columns = pl.ds(pl.multiple_of(index * pair, pair), pair)
            keys = own_sums[layer, 0, :, columns] + peer_sums[layer, 0, :, columns]
            values = own_sums[layer, 1, :, columns] + peer_sums[layer, 1, :, columns]
            key_block = jnp.concatenate(
                [jnp.where(first, keys, zeros), jnp.where(first, zeros, keys)], axis=0
            ).astype(BF16)
            value_block = jnp.concatenate(
                [jnp.where(first, values, zeros), jnp.where(first, zeros, values)], axis=0
            ).astype(BF16)
            value_block = jnp.concatenate([value_block, counts], axis=1)

            def row_chunk(step, inner):
                piece = pl.ds(pl.multiple_of(step * attend_rows, attend_rows), attend_rows)
                scores = lax.dot_general(
                    query_rows[piece, columns],
                    key_block,
                    (((1,), (1,)), ((), ())),
                    preferred_element_type=F32,
                )
                probs = []
                for side in range(2):
                    part = scores[:, side * lat_count : (side + 1) * lat_count]
                    row_max = jnp.max(part, axis=-1, keepdims=True)
                    probs.append(jnp.exp(part - row_max).astype(BF16))
                mixed = jnp.dot(
                    jnp.concatenate(probs, axis=1), value_block, preferred_element_type=F32
                )
                attended[piece, columns] = (mixed[:, :pair] / mixed[:, pair:]).astype(BF16)
                return inner

            if attend_rows == rows:
                row_chunk(0, 0)
            else:
                lax.fori_loop(0, rows // attend_rows, row_chunk, 0)
            return carry

        lax.fori_loop(0, HEADS // 2, heads, 0)

    local[0].wait()
    layer_norm(0)

    own_latents.wait()

    def take_latents(step, carry):
        source = lax.rem(me + devices - step, devices)
        pltpu.make_async_remote_copy(
            src_ref=lat.at[source],
            dst_ref=lat.at[source],
            send_sem=lat_send_sem.at[step],
            recv_sem=lat_recv_sem.at[source],
            device_id=peer,
            device_id_type=MESH,
        ).wait_recv()
        return carry

    lax.fori_loop(1, devices, take_latents, 0)
    lat_rows[...] = lat[...].astype(F32).reshape(lat_count, half).astype(BF16)

    for layer in range(LAYERS):
        for index in range(2):
            own["kv"[index], layer].wait()
            project_latents(index, layer)
            sums_copy(index, layer).start()
        weight_copy(1, layer).start()
        if layer + 1 < LAYERS:
            weight_copy(0, layer + 1).start()

    for layer in range(LAYERS):
        if layer > 0:
            layer_norm(layer)
        own["q", layer].wait()
        weight_wait(weight_recv_sem, wq, 0, layer, n, half, weight_send_sem, peer)
        project_queries(layer)
        sums_copy(0, layer).wait_recv()
        sums_copy(1, layer).wait_recv()
        attend(layer)
        own["o", layer].wait()
        weight_wait(weight_recv_sem, wo, 1, layer, n, half, weight_send_sem, peer)
        project_output(layer, out if layer == LAYERS - 1 else hidden)

    def finish_latents(step, carry):
        latent_copy(step).wait_send()
        return carry

    lax.fori_loop(1, devices, finish_latents, 0)
    for layer in range(LAYERS):
        for index in range(2):
            weight_copy(index, layer).wait_send()
            sums_copy(index, layer).wait_send()


def weight_wait(recv_sem, target, index, layer, n, half, send_sem, peer):
    other_half = pl.ds(pl.multiple_of((1 - n) * half, half), half)
    pltpu.make_async_remote_copy(
        src_ref=target.at[layer, other_half],
        dst_ref=target.at[layer, other_half],
        send_sem=send_sem.at[index, layer],
        recv_sem=recv_sem.at[index, layer],
        device_id=peer,
        device_id_type=MESH,
    ).wait_recv()


def shards(wide, narrow, queries, latents, norm_gains, q_weight, k_weight, v_weight, o_weight):
    rows, width = queries.shape
    devices = wide * narrow
    lat_piece = latents.shape[0]
    lat_count = devices * lat_piece
    half = k_weight.shape[1]
    anywhere = pl.BlockSpec(memory_space=pl.ANY)
    vmem = pl.BlockSpec(memory_space=pltpu.VMEM)
    dma = pltpu.SemaphoreType.DMA
    return pl.pallas_call(
        functools.partial(decoder, wide, narrow),
        out_shape=jax.ShapeDtypeStruct((rows, width), BF16),
        in_specs=[anywhere, anywhere, vmem, anywhere, anywhere, anywhere, anywhere],
        out_specs=vmem,
        scratch_shapes=[
            pltpu.VMEM((rows, width), BF16),
            pltpu.VMEM((rows, width), BF16),
            pltpu.VMEM((rows, width), BF16),
            pltpu.VMEM((rows, width), BF16),
            pltpu.VMEM((devices, lat_piece, half), BF16),
            pltpu.VMEM((lat_count, half), BF16),
            pltpu.VMEM((LAYERS, narrow * half, width), BF16),
            pltpu.VMEM((LAYERS, narrow * half, width), BF16),
            pltpu.VMEM((LAYERS, half, width), BF16),
            pltpu.VMEM((LAYERS, half, width), BF16),
            pltpu.VMEM((LAYERS, 2, lat_count, width), F32),
            pltpu.VMEM((LAYERS, 2, lat_count, width), F32),
            dma,
            dma,
            dma((4, LAYERS)),
            dma((devices,)),
            dma((devices,)),
            dma((2, LAYERS)),
            dma((2, LAYERS)),
            dma((2, LAYERS)),
            dma((2, LAYERS)),
        ],
        compiler_params=pltpu.CompilerParams(
            collective_id=0,
            has_side_effects=True,
            vmem_limit_bytes=60 * 1024 * 1024,
        ),
    )(queries, latents, norm_gains, q_weight, k_weight, v_weight, o_weight)


def solution(mesh):
    rows = P(("groups", "wide", "narrow"), None)
    panel = P(None, "narrow", None)
    return jax.shard_map(
        functools.partial(shards, mesh.shape["wide"], mesh.shape["narrow"]),
        mesh=mesh,
        in_specs=(rows, rows, P(), panel, panel, panel, panel),
        out_specs=rows,
        check_vma=False,
    )
```

```python
import functools

import jax
import jax.numpy as jnp
from jax import lax
from jax.experimental import pallas as pl
from jax.experimental.pallas import tpu as pltpu
from jax.sharding import PartitionSpec as P

HEADS = 16
LAYERS = 2
MESH = pl.DeviceIdType.MESH
F32 = jnp.float32
BF16 = jnp.bfloat16


def decoder(
    wide,
    narrow,
    queries,
    latents,
    gains,
    q_weight,
    k_weight,
    v_weight,
    o_weight,
    out,
    hidden,
    normed,
    query_rows,
    attended,
    lat,
    lat_rows,
    wq,
    wo,
    wk,
    wv,
    own_sums,
    peer_sums,
    local_sem,
    lat_local_sem,
    weight_local_sem,
    lat_send_sem,
    lat_recv_sem,
    weight_send_sem,
    weight_recv_sem,
    sums_send_sem,
    sums_recv_sem,
):
    devices = wide * narrow
    w = lax.axis_index("wide")
    n = lax.axis_index("narrow")
    me = w * narrow + n
    rows, width = hidden.shape
    half = wk.shape[1]
    lat_count = lat_rows.shape[0]
    head_size = width // HEADS
    pair = 2 * head_size
    scale = head_size ** (-0.5)
    my_half = pl.ds(pl.multiple_of(n * half, half), half)
    peer = {"narrow": 1 - n}

    local = [pltpu.make_async_copy(queries, hidden, local_sem)]
    own_latents = pltpu.make_async_copy(latents.at[:, my_half], lat.at[me], lat_local_sem)
    own = {}
    for layer in range(LAYERS):
        own["q", layer] = pltpu.make_async_copy(
            q_weight.at[layer], wq.at[layer, my_half], weight_local_sem.at[0, layer]
        )
        own["o", layer] = pltpu.make_async_copy(
            o_weight.at[layer], wo.at[layer, my_half], weight_local_sem.at[1, layer]
        )
        own["k", layer] = pltpu.make_async_copy(
            k_weight.at[layer], wk.at[layer], weight_local_sem.at[2, layer]
        )
        own["v", layer] = pltpu.make_async_copy(
            v_weight.at[layer], wv.at[layer], weight_local_sem.at[3, layer]
        )
    local[0].start()
    own_latents.start()
    for layer in range(LAYERS):
        for name in "kvqo":
            own[name, layer].start()

    barrier = pltpu.get_barrier_semaphore()

    def greet(step, carry):
        other = lax.rem(me + step, devices)
        pl.semaphore_signal(
            barrier,
            inc=1,
            device_id={"wide": other // narrow, "narrow": lax.rem(other, narrow)},
            device_id_type=MESH,
        )
        return carry

    lax.fori_loop(1, devices, greet, 0)

    def latent_copy(step):
        other = lax.rem(me + step, devices)
        other_n = lax.rem(other, narrow)
        columns = pl.ds(pl.multiple_of(other_n * half, half), half)
        return pltpu.make_async_remote_copy(
            src_ref=latents.at[:, columns],
            dst_ref=lat.at[me],
            send_sem=lat_send_sem.at[step],
            recv_sem=lat_recv_sem.at[me],
            device_id={"wide": other // narrow, "narrow": other_n},
            device_id_type=MESH,
        )

    def send_latents(step, carry):
        latent_copy(step).start()
        return carry

    def weight_copy(index, layer):
        source, target = ((q_weight, wq), (o_weight, wo))[index]
        return pltpu.make_async_remote_copy(
            src_ref=source.at[layer],
            dst_ref=target.at[layer, my_half],
            send_sem=weight_send_sem.at[index, layer],
            recv_sem=weight_recv_sem.at[index, layer],
            device_id=peer,
            device_id_type=MESH,
        )

    def sums_copy(layer, col):
        return pltpu.make_async_remote_copy(
            src_ref=own_sums.at[layer, col],
            dst_ref=peer_sums.at[layer, col],
            send_sem=sums_send_sem.at[layer, col],
            recv_sem=sums_recv_sem.at[layer, col],
            device_id=peer,
            device_id_type=MESH,
        )

    norm_rows = min(rows, 128)

    def layer_norm(layer):
        gain = gains[layer : layer + 1, :]

        def chunk(index, carry):
            piece = pl.ds(pl.multiple_of(index * norm_rows, norm_rows), norm_rows)
            values = hidden[piece, :].astype(F32)
            center = values - jnp.mean(values, axis=-1, keepdims=True)
            spread = jnp.mean(center * center, axis=-1, keepdims=True)
            normed[piece, :] = (center * lax.rsqrt(spread + 1e-05) * gain).astype(BF16)
            return carry

        lax.fori_loop(0, rows // norm_rows, chunk, 0)

    sum_rows = min(lat_count, 256)
    tile = 256
    tiles = width // tile

    def project_latents(layer, col):
        columns = pl.ds(col * tile, tile)

        def chunk(step, carry):
            piece = pl.ds(step * sum_rows if isinstance(step, int) else pl.multiple_of(step * sum_rows, sum_rows), sum_rows)
            for index in range(2):
                own_sums[layer, col, index, piece, :] = jnp.dot(
                    lat_rows[piece, :], (wk, wv)[index][layer, :, columns], preferred_element_type=F32
                )
            return carry

        loop(lat_count // sum_rows, chunk)

    def project_queries(layer):
        def chunk(col, carry):
            columns = pl.ds(pl.multiple_of(col * tile, tile), tile)
            sums = jnp.dot(normed[...], wq[layer, :, columns], preferred_element_type=F32)
            query_rows[:, columns] = (sums * scale).astype(BF16)
            return carry

        lax.fori_loop(0, width // tile, chunk, 0)

    def project_output(layer, target):
        def chunk(col, carry):
            columns = pl.ds(pl.multiple_of(col * tile, tile), tile)
            sums = jnp.dot(attended[...], wo[layer, :, columns], preferred_element_type=F32)
            target[:, columns] = (hidden[:, columns].astype(F32) + sums).astype(BF16)
            return carry

        lax.fori_loop(0, width // tile, chunk, 0)

    attend_rows = min(rows, 256 if lat_count <= 256 else 128)
    first = lax.broadcasted_iota(jnp.int32, (lat_count, pair), 1) < head_size
    zeros = jnp.zeros((lat_count, pair), F32)
    ones = jnp.ones((lat_count, pair), F32)
    counts = jnp.concatenate(
        [jnp.where(first, ones, zeros), jnp.where(first, zeros, ones)], axis=0
    ).astype(BF16)

    def attend_pair(layer, col, at):
        columns = pl.ds(col * tile + at, pair)
        keys = own_sums[layer, col, 0, :, at : at + pair] + peer_sums[layer, col, 0, :, at : at + pair]
        values = own_sums[layer, col, 1, :, at : at + pair] + peer_sums[layer, col, 1, :, at : at + pair]
        key_block = jnp.concatenate(
            [jnp.where(first, keys, zeros), jnp.where(first, zeros, keys)], axis=0
        ).astype(BF16)
        value_block = jnp.concatenate(
            [jnp.where(first, values, zeros), jnp.where(first, zeros, values)], axis=0
        ).astype(BF16)
        value_block = jnp.concatenate([value_block, counts], axis=1)

        def row_chunk(step, carry):
            piece = pl.ds(step * attend_rows if isinstance(step, int) else pl.multiple_of(step * attend_rows, attend_rows), attend_rows)
            scores = lax.dot_general(
                query_rows[piece, columns],
                key_block,
                (((1,), (1,)), ((), ())),
                preferred_element_type=F32,
            )
            probs = []
            for side in range(2):
                part = scores[:, side * lat_count : (side + 1) * lat_count]
                row_max = jnp.max(part, axis=-1, keepdims=True)
                probs.append(jnp.exp(part - row_max).astype(BF16))
            mixed = jnp.dot(
                jnp.concatenate(probs, axis=1), value_block, preferred_element_type=F32
            )
            attended[piece, columns] = (mixed[:, :pair] / mixed[:, pair:]).astype(BF16)
            return carry

        loop(rows // attend_rows, row_chunk)

    local[0].wait()
    layer_norm(0)
    pl.semaphore_wait(barrier, devices - 1)
    lax.fori_loop(1, devices, send_latents, 0)
    weight_copy(0, 0).start()

    own["q", 0].wait()
    weight_wait(weight_recv_sem, wq, 0, 0, n, half, weight_send_sem, peer)
    weight_copy(1, 0).start()
    project_queries(0)

    own_latents.wait()

    def take_latents(step, carry):
        source = lax.rem(me + devices - step, devices)
        pltpu.make_async_remote_copy(
            src_ref=lat.at[source],
            dst_ref=lat.at[source],
            send_sem=lat_send_sem.at[step],
            recv_sem=lat_recv_sem.at[source],
            device_id=peer,
            device_id_type=MESH,
        ).wait_recv()
        return carry

    lax.fori_loop(1, devices, take_latents, 0)
    lat_rows[...] = lat[...].astype(F32).reshape(lat_count, half).astype(BF16)

    for layer in range(LAYERS):
        own["k", layer].wait()
        own["v", layer].wait()
        for col in range(tiles):
            project_latents(layer, col)
            if layer == 0:
                sums_copy(layer, col).start()

    for layer in range(LAYERS):
        if layer > 0:
            layer_norm(layer)
            own["q", layer].wait()
            weight_wait(weight_recv_sem, wq, 0, layer, n, half, weight_send_sem, peer)
            project_queries(layer)
        for col in range(tiles):
            sums_copy(layer, col).wait_recv()
            if col == tiles // 2 and layer + 1 < LAYERS:
                weight_copy(0, layer + 1).start()
                for later in range(tiles):
                    sums_copy(layer + 1, later).start()
                weight_copy(1, layer + 1).start()
            for at in range(0, tile, pair):
                attend_pair(layer, col, at)
        own["o", layer].wait()
        weight_wait(weight_recv_sem, wo, 1, layer, n, half, weight_send_sem, peer)
        project_output(layer, out if layer == LAYERS - 1 else hidden)

    def finish_latents(step, carry):
        latent_copy(step).wait_send()
        return carry

    lax.fori_loop(1, devices, finish_latents, 0)
    for layer in range(LAYERS):
        for index in range(2):
            weight_copy(index, layer).wait_send()
        for col in range(tiles):
            sums_copy(layer, col).wait_send()


def loop(count, body):
    if count <= 2:
        for step in range(count):
            body(step, 0)
    else:
        lax.fori_loop(0, count, body, 0)


def weight_wait(recv_sem, target, index, layer, n, half, send_sem, peer):
    other_half = pl.ds(pl.multiple_of((1 - n) * half, half), half)
    pltpu.make_async_remote_copy(
        src_ref=target.at[layer, other_half],
        dst_ref=target.at[layer, other_half],
        send_sem=send_sem.at[index, layer],
        recv_sem=recv_sem.at[index, layer],
        device_id=peer,
        device_id_type=MESH,
    ).wait_recv()


def shards(wide, narrow, queries, latents, norm_gains, q_weight, k_weight, v_weight, o_weight):
    rows, width = queries.shape
    devices = wide * narrow
    lat_piece = latents.shape[0]
    lat_count = devices * lat_piece
    half = k_weight.shape[1]
    anywhere = pl.BlockSpec(memory_space=pl.ANY)
    vmem = pl.BlockSpec(memory_space=pltpu.VMEM)
    dma = pltpu.SemaphoreType.DMA
    return pl.pallas_call(
        functools.partial(decoder, wide, narrow),
        out_shape=jax.ShapeDtypeStruct((rows, width), BF16),
        in_specs=[anywhere, anywhere, vmem, anywhere, anywhere, anywhere, anywhere],
        out_specs=vmem,
        scratch_shapes=[
            pltpu.VMEM((rows, width), BF16),
            pltpu.VMEM((rows, width), BF16),
            pltpu.VMEM((rows, width), BF16),
            pltpu.VMEM((rows, width), BF16),
            pltpu.VMEM((devices, lat_piece, half), BF16),
            pltpu.VMEM((lat_count, half), BF16),
            pltpu.VMEM((LAYERS, narrow * half, width), BF16),
            pltpu.VMEM((LAYERS, narrow * half, width), BF16),
            pltpu.VMEM((LAYERS, half, width), BF16),
            pltpu.VMEM((LAYERS, half, width), BF16),
            pltpu.VMEM((LAYERS, width // 256, 2, lat_count, 256), F32),
            pltpu.VMEM((LAYERS, width // 256, 2, lat_count, 256), F32),
            dma,
            dma,
            dma((4, LAYERS)),
            dma((devices,)),
            dma((devices,)),
            dma((2, LAYERS)),
            dma((2, LAYERS)),
            dma((LAYERS, width // 256)),
            dma((LAYERS, width // 256)),
        ],
        compiler_params=pltpu.CompilerParams(
            collective_id=0,
            has_side_effects=True,
            vmem_limit_bytes=60 * 1024 * 1024,
        ),
    )(queries, latents, norm_gains, q_weight, k_weight, v_weight, o_weight)


def solution(mesh):
    rows = P(("groups", "wide", "narrow"), None)
    panel = P(None, "narrow", None)
    return jax.shard_map(
        functools.partial(shards, mesh.shape["wide"], mesh.shape["narrow"]),
        mesh=mesh,
        in_specs=(rows, rows, P(), panel, panel, panel, panel),
        out_specs=rows,
        check_vma=False,
    )
```

```python
import functools

import jax
import jax.numpy as jnp
from jax import lax
from jax.experimental import pallas as pl
from jax.experimental.pallas import tpu as pltpu
from jax.sharding import PartitionSpec as P

HEADS = 16
LAYERS = 2
MESH = pl.DeviceIdType.MESH
F32 = jnp.float32
BF16 = jnp.bfloat16


def decoder(
    wide,
    narrow,
    queries,
    latents,
    gains,
    q_weight,
    k_weight,
    v_weight,
    o_weight,
    out,
    hidden,
    normed,
    query_rows,
    attended,
    lat,
    lat_rows,
    wq,
    wo,
    wk,
    wv,
    own_sums,
    peer_sums,
    local_sem,
    lat_local_sem,
    weight_local_sem,
    lat_send_sem,
    lat_recv_sem,
    weight_send_sem,
    weight_recv_sem,
    sums_send_sem,
    sums_recv_sem,
    out_sem,
):
    devices = wide * narrow
    w = lax.axis_index("wide")
    n = lax.axis_index("narrow")
    me = w * narrow + n
    rows, width = hidden.shape
    half = wk.shape[1]
    lat_count = lat_rows.shape[0]
    head_size = width // HEADS
    pair = 2 * head_size
    scale = head_size ** (-0.5)
    my_half = pl.ds(pl.multiple_of(n * half, half), half)
    peer = {"narrow": 1 - n}

    local = [pltpu.make_async_copy(queries, hidden, local_sem)]
    own_latents = pltpu.make_async_copy(latents.at[:, my_half], lat.at[me], lat_local_sem)
    own = {}
    for layer in range(LAYERS):
        own["q", layer] = pltpu.make_async_copy(
            q_weight.at[layer], wq.at[layer, my_half], weight_local_sem.at[0, layer]
        )
        own["o", layer] = pltpu.make_async_copy(
            o_weight.at[layer], wo.at[layer, my_half], weight_local_sem.at[1, layer]
        )
        own["k", layer] = pltpu.make_async_copy(
            k_weight.at[layer], wk.at[layer], weight_local_sem.at[2, layer]
        )
        own["v", layer] = pltpu.make_async_copy(
            v_weight.at[layer], wv.at[layer], weight_local_sem.at[3, layer]
        )
    local[0].start()
    own_latents.start()
    for layer in range(LAYERS):
        for name in "kvqo":
            own[name, layer].start()

    barrier = pltpu.get_barrier_semaphore()

    def greet(step, carry):
        other = lax.rem(me + step, devices)
        pl.semaphore_signal(
            barrier,
            inc=1,
            device_id={"wide": other // narrow, "narrow": lax.rem(other, narrow)},
            device_id_type=MESH,
        )
        return carry

    lax.fori_loop(1, devices, greet, 0)

    def latent_copy(step):
        other = lax.rem(me + step, devices)
        other_n = lax.rem(other, narrow)
        columns = pl.ds(pl.multiple_of(other_n * half, half), half)
        return pltpu.make_async_remote_copy(
            src_ref=latents.at[:, columns],
            dst_ref=lat.at[me],
            send_sem=lat_send_sem.at[step],
            recv_sem=lat_recv_sem.at[me],
            device_id={"wide": other // narrow, "narrow": other_n},
            device_id_type=MESH,
        )

    def send_latents(step, carry):
        latent_copy(step).start()
        return carry

    def weight_copy(index, layer):
        source, target = ((q_weight, wq), (o_weight, wo))[index]
        return pltpu.make_async_remote_copy(
            src_ref=source.at[layer],
            dst_ref=target.at[layer, my_half],
            send_sem=weight_send_sem.at[index, layer],
            recv_sem=weight_recv_sem.at[index, layer],
            device_id=peer,
            device_id_type=MESH,
        )

    def sums_copy(layer, col):
        return pltpu.make_async_remote_copy(
            src_ref=own_sums.at[layer, col],
            dst_ref=peer_sums.at[layer, col],
            send_sem=sums_send_sem.at[layer, col],
            recv_sem=sums_recv_sem.at[layer, col],
            device_id=peer,
            device_id_type=MESH,
        )

    norm_rows = min(rows, 128)

    def layer_norm(layer):
        gain = gains[layer : layer + 1, :]

        def chunk(index, carry):
            piece = pl.ds(pl.multiple_of(index * norm_rows, norm_rows), norm_rows)
            values = hidden[piece, :].astype(F32)
            center = values - jnp.mean(values, axis=-1, keepdims=True)
            spread = jnp.mean(center * center, axis=-1, keepdims=True)
            normed[piece, :] = (center * lax.rsqrt(spread + 1e-05) * gain).astype(BF16)
            return carry

        lax.fori_loop(0, rows // norm_rows, chunk, 0)

    sum_rows = min(lat_count, 256)
    tile = 256
    tiles = width // tile

    def project_latents(layer, col):
        columns = pl.ds(col * tile, tile)

        def chunk(step, carry):
            piece = pl.ds(step * sum_rows if isinstance(step, int) else pl.multiple_of(step * sum_rows, sum_rows), sum_rows)
            for index in range(2):
                own_sums[layer, col, index, piece, :] = jnp.dot(
                    lat_rows[piece, :], (wk, wv)[index][layer, :, columns], preferred_element_type=F32
                )
            return carry

        loop(lat_count // sum_rows, chunk)

    def project_queries(layer):
        def chunk(col, carry):
            columns = pl.ds(pl.multiple_of(col * tile, tile), tile)
            sums = jnp.dot(normed[...], wq[layer, :, columns], preferred_element_type=F32)
            query_rows[:, columns] = (sums * scale).astype(BF16)
            return carry

        lax.fori_loop(0, width // tile, chunk, 0)

    def out_copy(col):
        columns = pl.ds(col * tile, tile)
        return pltpu.make_async_copy(hidden.at[:, columns], out.at[:, columns], out_sem.at[col])

    def project_output(layer):
        for col in range(tiles):
            columns = pl.ds(col * tile, tile)
            sums = jnp.dot(attended[...], wo[layer, :, columns], preferred_element_type=F32)
            hidden[:, columns] = (hidden[:, columns].astype(F32) + sums).astype(BF16)
            if layer == LAYERS - 1:
                out_copy(col).start()

    attend_rows = min(rows, 256 if lat_count <= 256 else 128)
    first = lax.broadcasted_iota(jnp.int32, (lat_count, pair), 1) < head_size
    zeros = jnp.zeros((lat_count, pair), F32)
    ones = jnp.ones((lat_count, pair), F32)
    counts = jnp.concatenate(
        [jnp.where(first, ones, zeros), jnp.where(first, zeros, ones)], axis=0
    ).astype(BF16)

    def attend_pair(layer, col, at):
        columns = pl.ds(col * tile + at, pair)
        keys = own_sums[layer, col, 0, :, at : at + pair] + peer_sums[layer, col, 0, :, at : at + pair]
        values = own_sums[layer, col, 1, :, at : at + pair] + peer_sums[layer, col, 1, :, at : at + pair]
        key_block = jnp.concatenate(
            [jnp.where(first, keys, zeros), jnp.where(first, zeros, keys)], axis=0
        ).astype(BF16)
        value_block = jnp.concatenate(
            [jnp.where(first, values, zeros), jnp.where(first, zeros, values)], axis=0
        ).astype(BF16)
        value_block = jnp.concatenate([value_block, counts], axis=1)

        def row_chunk(step, carry):
            piece = pl.ds(step * attend_rows if isinstance(step, int) else pl.multiple_of(step * attend_rows, attend_rows), attend_rows)
            scores = lax.dot_general(
                query_rows[piece, columns],
                key_block,
                (((1,), (1,)), ((), ())),
                preferred_element_type=F32,
            )
            probs = []
            for side in range(2):
                part = scores[:, side * lat_count : (side + 1) * lat_count]
                row_max = jnp.max(part, axis=-1, keepdims=True)
                probs.append(jnp.exp(part - row_max).astype(BF16))
            mixed = jnp.dot(
                jnp.concatenate(probs, axis=1), value_block, preferred_element_type=F32
            )
            attended[piece, columns] = (mixed[:, :pair] / mixed[:, pair:]).astype(BF16)
            return carry

        loop(rows // attend_rows, row_chunk)

    local[0].wait()
    layer_norm(0)
    pl.semaphore_wait(barrier, devices - 1)
    lax.fori_loop(1, devices, send_latents, 0)
    weight_copy(0, 0).start()

    own["q", 0].wait()
    weight_wait(weight_recv_sem, wq, 0, 0, n, half, weight_send_sem, peer)
    weight_copy(1, 0).start()
    project_queries(0)

    own_latents.wait()

    def take_latents(step, carry):
        source = lax.rem(me + devices - step, devices)
        pltpu.make_async_remote_copy(
            src_ref=lat.at[source],
            dst_ref=lat.at[source],
            send_sem=lat_send_sem.at[step],
            recv_sem=lat_recv_sem.at[source],
            device_id=peer,
            device_id_type=MESH,
        ).wait_recv()
        return carry

    lax.fori_loop(1, devices, take_latents, 0)
    lat_rows[...] = lat[...].astype(F32).reshape(lat_count, half).astype(BF16)

    for layer in range(LAYERS):
        own["k", layer].wait()
        own["v", layer].wait()
        for col in range(tiles):
            project_latents(layer, col)
            if layer == 0:
                sums_copy(layer, col).start()

    for layer in range(LAYERS):
        if layer > 0:
            layer_norm(layer)
            own["q", layer].wait()
            weight_wait(weight_recv_sem, wq, 0, layer, n, half, weight_send_sem, peer)
            project_queries(layer)
        for col in range(tiles):
            sums_copy(layer, col).wait_recv()
            if col == tiles // 2 and layer + 1 < LAYERS:
                weight_copy(0, layer + 1).start()
                for later in range(tiles):
                    sums_copy(layer + 1, later).start()
                weight_copy(1, layer + 1).start()
            for at in range(0, tile, pair):
                attend_pair(layer, col, at)
        own["o", layer].wait()
        weight_wait(weight_recv_sem, wo, 1, layer, n, half, weight_send_sem, peer)
        project_output(layer)

    def finish_latents(step, carry):
        latent_copy(step).wait_send()
        return carry

    lax.fori_loop(1, devices, finish_latents, 0)
    for layer in range(LAYERS):
        for index in range(2):
            weight_copy(index, layer).wait_send()
        for col in range(tiles):
            sums_copy(layer, col).wait_send()
    for col in range(tiles):
        out_copy(col).wait()


def loop(count, body):
    if count <= 2:
        for step in range(count):
            body(step, 0)
    else:
        lax.fori_loop(0, count, body, 0)


def weight_wait(recv_sem, target, index, layer, n, half, send_sem, peer):
    other_half = pl.ds(pl.multiple_of((1 - n) * half, half), half)
    pltpu.make_async_remote_copy(
        src_ref=target.at[layer, other_half],
        dst_ref=target.at[layer, other_half],
        send_sem=send_sem.at[index, layer],
        recv_sem=recv_sem.at[index, layer],
        device_id=peer,
        device_id_type=MESH,
    ).wait_recv()


def shards(wide, narrow, queries, latents, norm_gains, q_weight, k_weight, v_weight, o_weight):
    rows, width = queries.shape
    devices = wide * narrow
    lat_piece = latents.shape[0]
    lat_count = devices * lat_piece
    half = k_weight.shape[1]
    anywhere = pl.BlockSpec(memory_space=pl.ANY)
    vmem = pl.BlockSpec(memory_space=pltpu.VMEM)
    dma = pltpu.SemaphoreType.DMA
    return pl.pallas_call(
        functools.partial(decoder, wide, narrow),
        out_shape=jax.ShapeDtypeStruct((rows, width), BF16),
        in_specs=[anywhere, anywhere, vmem, anywhere, anywhere, anywhere, anywhere],
        out_specs=anywhere,
        scratch_shapes=[
            pltpu.VMEM((rows, width), BF16),
            pltpu.VMEM((rows, width), BF16),
            pltpu.VMEM((rows, width), BF16),
            pltpu.VMEM((rows, width), BF16),
            pltpu.VMEM((devices, lat_piece, half), BF16),
            pltpu.VMEM((lat_count, half), BF16),
            pltpu.VMEM((LAYERS, narrow * half, width), BF16),
            pltpu.VMEM((LAYERS, narrow * half, width), BF16),
            pltpu.VMEM((LAYERS, half, width), BF16),
            pltpu.VMEM((LAYERS, half, width), BF16),
            pltpu.VMEM((LAYERS, width // 256, 2, lat_count, 256), F32),
            pltpu.VMEM((LAYERS, width // 256, 2, lat_count, 256), F32),
            dma,
            dma,
            dma((4, LAYERS)),
            dma((devices,)),
            dma((devices,)),
            dma((2, LAYERS)),
            dma((2, LAYERS)),
            dma((LAYERS, width // 256)),
            dma((LAYERS, width // 256)),
            dma((width // 256,)),
        ],
        compiler_params=pltpu.CompilerParams(
            collective_id=0,
            has_side_effects=True,
            vmem_limit_bytes=60 * 1024 * 1024,
        ),
    )(queries, latents, norm_gains, q_weight, k_weight, v_weight, o_weight)


def solution(mesh):
    rows = P(("groups", "wide", "narrow"), None)
    panel = P(None, "narrow", None)
    return jax.shard_map(
        functools.partial(shards, mesh.shape["wide"], mesh.shape["narrow"]),
        mesh=mesh,
        in_specs=(rows, rows, P(), panel, panel, panel, panel),
        out_specs=rows,
        check_vma=False,
    )
```
